512 devices in a mesh: teach: 16 (over x, y), stud: 8 (over z_lo, core), mdl: 4 (over z_hi).
Axes of the slice: x: 4, y: 4, z: 16 (z_hi: 4, z_lo: 4; z = z_hi * 4 + z_lo), core: 2. Of those that a mesh axis runs over, the one named last changes fastest.
Arguments:
- states: bfloat16 [16384, 512], P(('teach', 'stud')), may hold values from -6 to 6
- task_ids: int32 [16384, 1], P(('teach', 'stud')), may hold values from 0 to 15; in each aligned block of 128 rows (0 to 127, 128 to 255, ...) at most 12 rows name the same one
- student_batch: int32 [16384, 1], P(('teach', 'stud')), may hold values from 0 to 127; in each aligned block of 128 rows (0 to 127, 128 to 255, ...) at most 2 rows name the same one
- teach_in: bfloat16 [16, 512, 1024], P('teach', None, 'mdl'), may hold values from -0.25 to 0.25
- teach_out: bfloat16 [16, 1024, 512], P('teach', 'mdl'), may hold values from -0.1875 to 0.1875
- student_up: bfloat16 [512, 1024], P(None, 'mdl'), may hold values from -0.25 to 0.25
- student_down: bfloat16 [512, 1024], P(None, 'mdl'), may hold values from -0.1875 to 0.1875
Outputs:
- grad_up: float32 [512, 1024], P(('teach', 'stud'), 'mdl')
- grad_down: float32 [512, 1024], P(('teach', 'stud'), 'mdl')
The draws below stay inside these ranges and needn't reach their ends.
Inputs may be any that keep to these rules, and one draw needn't show every extreme that they name: `task_ids`: teacher t lives at index t // 1 of teach. Among one device's 128 states no teacher is named more than 12 times, and in every draw some teacher is named exactly 12 times there; every teacher is named somewhere. `student_batch`: batch b belongs to teach index b // 8 and stud index b % 8. Among one device's 128 states no batch is named more than 2 times, some batch exactly 2 times; every batch holds one state or more.
All inputs are finite; a program needn't handle non-finite values.
Results may differ from the reference program's by a relative error of at most 0.0023.
Values may be sent and summed in bfloat16 or wider, within the bound.
A program may use at most 64 MiB of HBM per device.

```python
import math
import jax
import jax.numpy as jnp
import numpy as np
from jax import lax

DS = 512
TW = 1024
HS = 1024
ACT = 512
ROWS = 128
NTEACH = 16
NB = 128
STATES = 16384
CAPT = 12
CAP2 = 2


def steps_of(own_key, extent, cuts, low, high):
    def one(position, parts):
        draws = jax.random.uniform(jax.random.fold_in(jax.random.fold_in(own_key, 6), position), (parts,), jnp.float32, low / len(cuts), high / len(cuts))
        return jnp.repeat(jnp.exp(draws), extent[position] // parts).reshape((-1,) + (1,) * (len(extent) - position - 1))

    level = one(*cuts[0])
    for cut in cuts[1:]:
        level = level * one(*cut)
    return level


def deal_out(own_key, own, number, rows, number_of, top, most, slope):
    order = jax.random.permutation(own_key, number_of)
    packed, common = load_shares(number_of, rows * top, most, slope, True), load_shares(number_of, rows * top, most, slope, False)
    places = jnp.arange(number_of)

    def named(tallies, offset_by):
        used = int((tallies > 0).sum())
        fixed = max(1, used // 4)
        moved = fixed + (places - fixed + offset_by * (used - fixed)) % max(1, number_of - fixed)
        return jnp.zeros((number_of,), jnp.int32).at[order[jnp.where(places < fixed, places, moved)]].set(jnp.asarray(tallies, jnp.int32))

    tallies = jnp.where(number % 4 == 0, named(packed, number // 4), named(common, number - number // 4 - 1))
    mixed = jax.random.permutation(jax.random.fold_in(own, 3), number_of)
    giver, sink = mixed[0:number_of // 2 * 2:2], mixed[1:number_of // 2 * 2:2]
    room = jnp.minimum(tallies[giver] - 1, most - tallies[sink]) // 2
    room = jnp.where((giver == order[0]) | (sink == order[0]) | (tallies[sink] == 0), 0, jnp.maximum(room, 0))
    moved = jax.random.randint(jax.random.fold_in(own, 4), (number_of // 2,), 0, 1 << 20) % (room + 1)
    tallies = tallies.at[giver].add(-moved).at[sink].add(moved)
    members = jnp.searchsorted(jnp.cumsum(tallies), jnp.arange(rows * top), side="right").astype(jnp.int32)
    listing = members.reshape(top, rows).T
    listing = listing[jax.random.permutation(jax.random.fold_in(own, 1), rows)]
    offset_by = jax.random.randint(jax.random.fold_in(own, 2), (rows, 1), 0, top)
    return jnp.take_along_axis(listing, (jnp.arange(top)[None, :] + offset_by) % top, axis=1)


def load_shares(number_of, total, bound, lean, full):
    portions = [(1 << 20) // math.isqrt(grade ** lean) + 1 for grade in range(1, number_of + 1)]
    largest = bound if full else min(bound, max(-(-total // number_of), total * portions[0] // sum(portions)))
    least = 1 if total - largest >= number_of - 1 else 0
    given, spare = [largest] + [least] * (number_of - 1), total - largest - least * (number_of - 1)
    while spare > 0:
        movable = [i for i in range(1, number_of) if given[i] < largest] or [i for i in range(1, number_of) if given[i] < bound]
        whole, budget = sum([portions[i] for i in movable]), spare
        for i in movable:
            addition = min(bound - given[i], max(1, budget * portions[i] // whole), spare)
            given[i] = given[i] + addition
            spare = spare - addition
    return np.array(given)


def noise(stream_key, dims, width, limit, shards=(), kind=jnp.bfloat16):
    array = jax.random.normal(stream_key, dims, jnp.float32) * width
    if len(shards) > 0:
        array = steps_of(stream_key, dims, shards, -0.22, 0.18) * array
    return jnp.clip(array, min=-limit, max=limit).astype(kind)


def setup_inputs(seed: int = 0) -> dict:
    arg_keys = jax.random.split(jax.random.key(seed), 8)
    states = noise(arg_keys[0], (STATES, DS), 1.0, 6.0, ((0, 128),))
    task_ids_keys = jax.random.split(jax.random.fold_in(arg_keys[1], 1), STATES // ROWS)
    task_ids_turns = jax.random.permutation(jax.random.fold_in(arg_keys[1], 3), STATES // ROWS)
    task_ids = jax.vmap(lambda own, number: deal_out(jax.random.fold_in(arg_keys[1], 2), own, number, ROWS, NTEACH, 1, CAPT, 2))(task_ids_keys, task_ids_turns).reshape((STATES, 1))
    student_batch_keys = jax.random.split(jax.random.fold_in(arg_keys[2], 1), STATES // ROWS)
    student_batch_turns = jax.random.permutation(jax.random.fold_in(arg_keys[2], 3), STATES // ROWS)
    student_batch = jax.vmap(lambda own, number: deal_out(jax.random.fold_in(arg_keys[2], 2), own, number, ROWS, NB, 1, CAP2, 2))(student_batch_keys, student_batch_turns).reshape((STATES, 1))
    teach_in = noise(arg_keys[3], (NTEACH, DS, TW), DS ** -0.5, 0.25, ((0, 16), (2, 4)))
    teach_out = noise(arg_keys[4], (NTEACH, TW, ACT), TW ** -0.5, 0.1875, ((0, 16), (1, 4)))
    student_up = noise(arg_keys[5], (DS, HS), DS ** -0.5, 0.25, ((1, 4),))
    student_down = noise(arg_keys[6], (ACT, HS), HS ** -0.5, 0.1875, ((1, 4),))
    return {"states": states, "task_ids": task_ids, "student_batch": student_batch, "teach_in": teach_in, "teach_out": teach_out, "student_up": student_up, "student_down": student_down}


def silu_slope(value):
    sig = jax.nn.sigmoid(value)
    return sig * (1.0 + value * (1.0 - sig))


def reference(states, task_ids, student_batch, teach_in, teach_out, student_up, student_down):
    task_list = task_ids[:, 0]
    batch_list = student_batch[:, 0]
    room = NB * CAPT

    def one_teacher(index):
        chosen = task_list == index
        picked = jnp.nonzero(chosen, size=room, fill_value=0)[0].astype(jnp.int32)
        live = (jnp.arange(room, dtype=jnp.int32) < jnp.sum(chosen.astype(jnp.int32))).astype(jnp.float32)
        rows_in = states[picked]
        hidden = jax.nn.silu(jnp.dot(rows_in, teach_in[index], preferred_element_type=jnp.float32)).astype(jnp.bfloat16)
        labels = jnp.dot(hidden, teach_out[index], preferred_element_type=jnp.float32) * live[:, None]
        return picked, labels

    picked, labels = lax.map(one_teacher, jnp.arange(NTEACH, dtype=jnp.int32))
    targets = jnp.zeros((STATES, ACT), labels.dtype).at[picked.reshape(-1)].add(labels.reshape(-1, ACT))
    counts = jnp.sum((batch_list[:, None] == jnp.arange(NB, dtype=jnp.int32)[None, :]).astype(jnp.float32), axis=0)
    weight = 2.0 / counts[batch_list]
    block = math.gcd(STATES, 4096)

    def accumulate(carry, index):
        grad_up, grad_down = carry
        start = index * block
        rows_in = lax.dynamic_slice_in_dim(states, start, block, 0)
        goal = lax.dynamic_slice_in_dim(targets, start, block, 0)
        scale = lax.dynamic_slice_in_dim(weight, start, block, 0)
        pre = jnp.dot(rows_in, student_up, preferred_element_type=jnp.float32)
        act = jax.nn.silu(pre).astype(jnp.bfloat16)
        pred = jnp.dot(act, student_down.T, preferred_element_type=jnp.float32)
        scaled = ((pred - goal) * scale[:, None]).astype(jnp.bfloat16)
        grad_down = grad_down + jnp.dot(scaled.T, act, preferred_element_type=jnp.float32)
        back = jnp.dot(scaled, student_down, preferred_element_type=jnp.float32)
        pre_grad = (back * silu_slope(pre)).astype(jnp.bfloat16)
        grad_up = grad_up + jnp.dot(rows_in.T, pre_grad, preferred_element_type=jnp.float32)
        return (grad_up, grad_down), None

    start_carry = (jnp.zeros((DS, HS), jnp.float32), jnp.zeros((ACT, HS), jnp.float32))
    (grad_up, grad_down), _ = lax.scan(accumulate, start_carry, jnp.arange(STATES // block, dtype=jnp.int32))
    return grad_up, grad_down
```

```python
import functools
import math

import jax
import jax.numpy as jnp
from jax import lax
from jax.experimental import pallas as pl
from jax.experimental.pallas import tpu as pltpu
from jax.sharding import PartitionSpec as P

MESH = pl.DeviceIdType.MESH
F32, BF16, I32 = jnp.float32, jnp.bfloat16, jnp.int32
ROOM = 12
BLOCK = 16
LANES = 128


def dot(a, b, ca=1, cb=0):
    return lax.dot_general(a, b, (((ca,), (cb,)), ((), ())), preferred_element_type=F32)


def iota(shape, dim):
    return lax.broadcasted_iota(I32, shape, dim)


def onehot(mask):
    return jnp.where(mask, 1.0, 0.0).astype(BF16)


def silu(value):
    return value * jax.nn.sigmoid(value)


def silu_slope(value):
    sig = jax.nn.sigmoid(value)
    return sig * (1.0 + value * (1.0 - sig))


def kernel(
    side,
    teachers,
    studs,
    states,
    tasks,
    batches,
    teach_in,
    teach_out,
    up,
    down,
    grad_up,
    grad_down,
    out,
    got,
    x,
    hid,
    act,
    pre,
    err,
    first_out,
    first_in,
    second_out,
    second_in,
    hist_out,
    hist_in,
    part_out,
    part_in,
    last_out,
    last_in,
    go_s,
    go_r,
    sum_s,
    sum_r,
    hist_s,
    hist_r,
    part_s,
    part_r,
    last_s,
    last_r,
):
    me_t, me_s, me_m = lax.axis_index("teach"), lax.axis_index("stud"), lax.axis_index("mdl")
    my_x, my_y = me_t // side, me_t % side
    rows, width = states.shape
    slots, used = teachers * BLOCK, teachers * ROOM
    pieces = width // LANES
    mates = (me_m + 1 - 2 * (me_m % 2), 3 - me_m)

    def hops(step):
        dx, dy = step // side, step % side
        return min(dx, side - dx) + min(dy, side - dy)

    steps = sorted(range(1, teachers), key=lambda step: -hops(step))

    def peer(step):
        return ((my_x + step // side) % side) * side + (my_y + step % side) % side

    barrier = pltpu.get_barrier_semaphore()
    for step in steps:
        pl.semaphore_signal(barrier, inc=1, device_id={"teach": peer(step)}, device_id_type=MESH)
    for step in range(1, studs):
        pl.semaphore_signal(
            barrier, inc=1, device_id={"stud": (me_s + step) % studs}, device_id_type=MESH
        )
    for mate in mates:
        pl.semaphore_signal(barrier, inc=1, device_id={"mdl": mate}, device_id_type=MESH)

    def send(src, dst, send_sem, recv_sem, where):
        copy = pltpu.make_async_remote_copy(
            src_ref=src,
            dst_ref=dst,
            send_sem=send_sem,
            recv_sem=recv_sem,
            device_id=where,
            device_id_type=MESH,
        )
        return copy

    hot = jnp.where(tasks[...] == iota((rows, teachers), 1), 1.0, 0.0)
    lower = onehot(iota((rows, rows), 0) > iota((rows, rows), 1))
    before = jnp.sum(dot(lower, hot.astype(BF16)) * hot, axis=1, keepdims=True)
    slot = tasks[...].astype(F32) * BLOCK + before
    slot = jnp.transpose(jnp.broadcast_to(slot, (rows, rows)))[0:1, :].astype(I32)
    note = ((slot >> 4) * BLOCK + ROOM + 1 + ((slot & 15) >> 2)) * 4 + (slot & 3)
    place = iota((slots, rows), 0)
    batch_hot = onehot(batches[...] == iota((rows, LANES), 1))
    dispatch = onehot(place == slot)
    for piece in range(pieces):
        noted = place * 4 + piece == note
        if piece == 0:
            noted = noted | ((place & 15) == ROOM)
        cols = slice(piece * LANES, (piece + 1) * LANES)
        block = dot(dispatch, states[:, cols]) + dot(onehot(noted), batch_hot)
        out[:, :, cols] = block.astype(BF16).reshape(teachers, BLOCK, LANES)

    pl.semaphore_wait(barrier, teachers - 1 + studs - 1 + 2)

    going = []
    for step in steps:
        to = peer(step)
        copy = send(
            out.at[to], got.at[me_t], go_s.at[step], go_r.at[step], {"teach": to}
        )
        copy.start()
        going.append(copy)
    got[me_t] = out[me_t]

    source = iota((used, slots), 1)
    target = iota((used, slots), 0)
    base, inner = (source >> 4) * ROOM, source & 15
    keep = onehot((target == base + inner) & (inner < ROOM))

    for copy in going:
        copy.wait_recv()

    arrived = got[...].reshape(slots, width)
    x[...] = dot(keep, arrived).astype(BF16)
    hid[...] = silu(dot(x[...], teach_in[0])).astype(BF16)
    pre[...] = dot(x[...], up[...])
    act[...] = silu(pre[...]).astype(BF16)

    order, firsts, seconds = [], [], []
    for turn in range(4):
        chunk = (my_x * 4 // side + 1 + turn) % 4
        cols = pl.ds(pl.multiple_of(chunk * LANES, LANES), LANES)
        order.append((chunk, cols))
        diff = dot(act[...], down[cols, :], 1, 1) - dot(hid[...], teach_out[0, :, cols])
        err[turn] = diff
        first_out[turn] = diff.astype(BF16)
        copy = send(
            first_out.at[turn],
            first_in.at[turn],
            sum_s.at[0, turn],
            sum_r.at[0, turn],
            {"mdl": mates[turn % 2]},
        )
        copy.start()
        firsts.append(copy)

    marks = onehot((iota((8, slots), 1) & 15) == ROOM)
    hist_out[...] = dot(marks, arrived[:, :LANES])
    hists = []
    for step in range(1, studs):
        to = (me_s + step) % studs
        copy = send(
            hist_out, hist_in.at[me_s], hist_s.at[step], hist_r.at[step], {"stud": to}
        )
        copy.start()
        hists.append(copy)
    hist_in[me_s] = hist_out[...]
    batch_of = jnp.zeros((used, LANES), F32)
    for piece in range(pieces):
        pick = onehot((target == base + (inner - ROOM - 1) * 4 + piece) & (inner > ROOM))
        batch_of += dot(pick, arrived[:, piece * LANES : (piece + 1) * LANES])
    pre[...] = silu_slope(pre[...])

    for turn in range(4):
        firsts[turn].wait_recv()
        diff = err[turn] + first_in[turn].astype(F32)
        err[turn] = diff
        second_out[turn] = diff.astype(BF16)
        copy = send(
            second_out.at[turn],
            second_in.at[turn],
            sum_s.at[1, turn],
            sum_r.at[1, turn],
            {"mdl": mates[1 - turn % 2]},
        )
        copy.start()
        seconds.append(copy)

    for copy in hists:
        copy.wait_recv()
    counts = jnp.sum(hist_in[...], axis=0)
    share = jnp.where(counts > 0.0, 2.0 / jnp.maximum(counts, 1.0), 0.0)
    weight = jnp.sum(batch_of * share[0:1, :], axis=1, keepdims=True)

    def part_copy(kind, to):
        return send(
            part_out.at[kind, to],
            part_in.at[kind, me_t],
            part_s.at[kind, to],
            part_r.at[kind, me_t],
            {"teach": to},
        )

    per = teachers // 4
    part_rows = part_out.shape[2]
    back = jnp.zeros((used, up.shape[1]), F32)
    for turn in range(4):
        chunk, cols = order[turn]
        seconds[turn].wait_recv()
        total = err[turn] + second_in[turn].astype(F32)
        scaled = (total * weight).astype(BF16)
        grad = dot(scaled, act[...], 0, 0)
        part_out[1, pl.ds(chunk * per, per)] = grad.astype(BF16).reshape(per, part_rows, -1)
        back += dot(scaled, down[cols, :])
        for piece in range(per):
            to = chunk * per + piece

            @pl.when(to != me_t)
            def _():
                part_copy(1, to).start()

    pre_grad = (back * pre[...]).astype(BF16)
    grad = dot(x[...], pre_grad, 0, 0)
    part_out[0] = grad.astype(BF16).reshape(teachers, part_rows, -1)
    for step in steps:
        part_copy(0, peer(step)).start()
    part_in[1, me_t] = part_out[1, me_t]
    part_in[0, me_t] = part_out[0, me_t]

    def part_wait(kind):
        for step in steps:
            source = peer(step)
            send(
                part_out.at[kind, source],
                part_in.at[kind, source],
                part_s.at[kind, source],
                part_r.at[kind, source],
                {"teach": source},
            ).wait_recv()
        return jnp.sum(part_in[kind].astype(F32), axis=0)

    chips = studs // 2
    sum_down = part_wait(1).reshape(chips, part_rows // chips, -1)
    sum_up = part_wait(0).reshape(chips, part_rows // chips, -1)
    last_out[...] = jnp.concatenate([sum_up, sum_down], axis=1).astype(BF16)
    lasts = []
    for step in range(1, studs):
        to = (me_s + step) % studs
        copy = send(
            last_out.at[to // 2],
            last_in.at[me_s],
            last_s.at[step],
            last_r.at[step],
            {"stud": to},
        )
        copy.start()
        lasts.append(copy)
    last_in[me_s] = last_out[me_s // 2]
    for copy in lasts:
        copy.wait_recv()
    total = jnp.sum(last_in[...].astype(F32), axis=0)
    mine = grad_up.shape[0]
    even = jnp.full(grad_up.shape, me_s % 2, I32) == 0
    grad_up[...] = jnp.where(even, total[0:mine], total[mine : 2 * mine])
    grad_down[...] = jnp.where(even, total[2 * mine : 3 * mine], total[3 * mine : 4 * mine])

    for copy in going + firsts + hists + seconds + lasts:
        copy.wait_send()
    for step in steps:
        for kind in range(2):
            part_copy(kind, peer(step)).wait_send()


def solution(mesh):
    teachers, studs = mesh.shape["teach"], mesh.shape["stud"]
    side = math.isqrt(teachers)

    def on_device(states, tasks, batches, teach_in, teach_out, up, down):
        width, part = up.shape
        actions = down.shape[0]
        slots, used = teachers * BLOCK, teachers * ROOM
        mine = width // (teachers * studs)
        vmem = pl.BlockSpec(memory_space=pltpu.VMEM)
        result = jax.ShapeDtypeStruct((mine, part), F32)
        dma = pltpu.SemaphoreType.DMA
        return pl.pallas_call(
            functools.partial(kernel, side, teachers, studs),
            out_shape=(result, result),
            in_specs=[vmem] * 7,
            out_specs=(vmem, vmem),
            scratch_shapes=[
                pltpu.VMEM((teachers, BLOCK, width), BF16),
                pltpu.VMEM((teachers, BLOCK, width), BF16),
                pltpu.VMEM((used, width), BF16),
                pltpu.VMEM((used, part), BF16),
                pltpu.VMEM((used, part), BF16),
                pltpu.VMEM((used, part), F32),
                pltpu.VMEM((4, used, actions // 4), F32),
                pltpu.VMEM((4, used, actions // 4), BF16),
                pltpu.VMEM((4, used, actions // 4), BF16),
                pltpu.VMEM((4, used, actions // 4), BF16),
                pltpu.VMEM((4, used, actions // 4), BF16),
                pltpu.VMEM((8, LANES), F32),
                pltpu.VMEM((studs, 8, LANES), F32),
                pltpu.VMEM((2, teachers, width // teachers, part), BF16),
                pltpu.VMEM((2, teachers, width // teachers, part), BF16),
                pltpu.VMEM((studs // 2, 4 * mine, part), BF16),
                pltpu.VMEM((studs, 4 * mine, part), BF16),
                dma((teachers,)),
                dma((teachers,)),
                dma((2, 4)),
                dma((2, 4)),
                dma((studs,)),
                dma((studs,)),
                dma((2, teachers)),
                dma((2, teachers)),
                dma((studs,)),
                dma((studs,)),
            ],
            compiler_params=pltpu.CompilerParams(collective_id=0, has_side_effects=True),
        )(states, tasks, batches, teach_in, teach_out, up, down)

    in_specs = (
        P(("teach", "stud"), None),
        P(("teach", "stud"), None),
        P(("teach", "stud"), None),
        P("teach", None, "mdl"),
        P("teach", "mdl", None),
        P(None, "mdl"),
        P(None, "mdl"),
    )
    out_specs = (P(("teach", "stud"), "mdl"), P(("teach", "stud"), "mdl"))
    return jax.shard_map(
        on_device, mesh=mesh, in_specs=in_specs, out_specs=out_specs, check_vma=False
    )
```

```python
import functools
import math

import jax
import jax.numpy as jnp
from jax import lax
from jax.experimental import pallas as pl
from jax.experimental.pallas import tpu as pltpu
from jax.sharding import PartitionSpec as P

MESH = pl.DeviceIdType.MESH
F32, BF16, I32 = jnp.float32, jnp.bfloat16, jnp.int32
ROOM = 12
BLOCK = 16
LANES = 128


def dot(a, b, ca=1, cb=0):
    return lax.dot_general(a, b, (((ca,), (cb,)), ((), ())), preferred_element_type=F32)


def iota(shape, dim):
    return lax.broadcasted_iota(I32, shape, dim)


def onehot(mask):
    return jnp.where(mask, 1.0, 0.0).astype(BF16)


def silu(value):
    return value * jax.nn.sigmoid(value)


def silu_slope(value):
    sig = jax.nn.sigmoid(value)
    return sig * (1.0 + value * (1.0 - sig))


def kernel(
    side,
    teachers,
    studs,
    states_hbm,
    tasks,
    batches,
    teach_in_hbm,
    teach_out_hbm,
    up_hbm,
    down_hbm,
    grads,
    states,
    teach_in,
    teach_out,
    up,
    down,
    out,
    got,
    x,
    hid,
    act,
    pre,
    err,
    first_out,
    first_in,
    second_out,
    second_in,
    hist_out,
    hist_in,
    part_out,
    part_in,
    last_out,
    last_in,
    load_s,
    go_s,
    go_r,
    sum_s,
    sum_r,
    hist_s,
    hist_r,
    part_s,
    part_r,
    last_s,
    last_r,
):
    me_t, me_s, me_m = lax.axis_index("teach"), lax.axis_index("stud"), lax.axis_index("mdl")
    my_x, my_y = me_t // side, me_t % side
    rows, width = states.shape
    slots, used = teachers * BLOCK, teachers * ROOM
    pieces = width // LANES
    mates = (me_m + 1 - 2 * (me_m % 2), 3 - me_m)

    def hops(step):
        dx, dy = step // side, step % side
        return min(dx, side - dx) + min(dy, side - dy)

    steps = sorted(range(1, teachers), key=lambda step: -hops(step))

    def peer(step):
        return ((my_x + step // side) % side) * side + (my_y + step % side) % side

    barrier = pltpu.get_barrier_semaphore()
    for step in steps:
        pl.semaphore_signal(barrier, inc=1, device_id={"teach": peer(step)}, device_id_type=MESH)
    for step in range(1, studs):
        pl.semaphore_signal(
            barrier, inc=1, device_id={"stud": (me_s + step) % studs}, device_id_type=MESH
        )
    for mate in mates:
        pl.semaphore_signal(barrier, inc=1, device_id={"mdl": mate}, device_id_type=MESH)

    def send(src, dst, send_sem, recv_sem, where):
        copy = pltpu.make_async_remote_copy(
            src_ref=src,
            dst_ref=dst,
            send_sem=send_sem,
            recv_sem=recv_sem,
            device_id=where,
            device_id_type=MESH,
        )
        return copy

    loads = []
    for index, (source, held) in enumerate(
        ((states_hbm, states), (teach_in_hbm, teach_in), (up_hbm, up), (down_hbm, down), (teach_out_hbm, teach_out))
    ):
        loads.append(pltpu.make_async_copy(source, held, load_s.at[index]))
        loads[-1].start()

    hot = jnp.where(tasks[...] == iota((teachers, rows), 0), 1.0, 0.0)
    earlier = onehot(iota((rows, rows), 0) < iota((rows, rows), 1))
    before = jnp.sum(dot(hot.astype(BF16), earlier) * hot, axis=0, keepdims=True)
    slot = tasks[...] * BLOCK + before.astype(I32)
    note = ((slot >> 4) * BLOCK + ROOM + 1 + ((slot & 15) >> 2)) * 4 + (slot & 3)
    place = iota((slots, rows), 0)
    batch_hot = onehot(batches[...] == iota((LANES, rows), 0))
    dispatch = onehot(place == slot)
    loads[0].wait()
    for piece in range(pieces):
        noted = place * 4 + piece == note
        if piece == 0:
            noted = noted | ((place & 15) == ROOM)
        cols = slice(piece * LANES, (piece + 1) * LANES)
        block = dot(dispatch, states[:, cols]) + dot(onehot(noted), batch_hot, 1, 1)
        out[:, :, cols] = block.astype(BF16).reshape(teachers, BLOCK, LANES)

    pl.semaphore_wait(barrier, teachers - 1 + studs - 1 + 2)

    going = []
    for step in steps:
        to = peer(step)
        copy = send(
            out.at[to], got.at[me_t], go_s.at[step], go_r.at[step], {"teach": to}
        )
        copy.start()
        going.append(copy)
    got[me_t] = out[me_t]

    source = iota((used, slots), 1)
    target = iota((used, slots), 0)
    base, inner = (source >> 4) * ROOM, source & 15
    keep = onehot((target == base + inner) & (inner < ROOM))

    for copy in going:
        copy.wait_recv()

    arrived = got[...].reshape(slots, width)
    for load in loads[1:]:
        load.wait()
    x[...] = dot(keep, arrived).astype(BF16)
    hid[...] = silu(dot(x[...], teach_in[0])).astype(BF16)
    pre[...] = dot(x[...], up[...])
    act[...] = silu(pre[...]).astype(BF16)

    order, firsts, seconds = [], [], []
    for turn in range(4):
        chunk = (my_x * 4 // side + 1 + turn) % 4
        cols = pl.ds(pl.multiple_of(chunk * LANES, LANES), LANES)
        order.append((chunk, cols))
        diff = dot(act[...], down[cols, :], 1, 1) - dot(hid[...], teach_out[0, :, cols])
        err[turn] = diff
        first_out[turn] = diff.astype(BF16)
        copy = send(
            first_out.at[turn],
            first_in.at[turn],
            sum_s.at[0, turn],
            sum_r.at[0, turn],
            {"mdl": mates[turn % 2]},
        )
        copy.start()
        firsts.append(copy)

    marks = onehot((iota((8, slots), 1) & 15) == ROOM)
    hist_out[...] = dot(marks, arrived[:, :LANES])
    hists = []
    for step in range(1, studs):
        to = (me_s + step) % studs
        copy = send(
            hist_out, hist_in.at[me_s], hist_s.at[step], hist_r.at[step], {"stud": to}
        )
        copy.start()
        hists.append(copy)
    hist_in[me_s] = hist_out[...]
    batch_of = jnp.zeros((used, LANES), F32)
    for piece in range(pieces):
        pick = onehot((target == base + (inner - ROOM - 1) * 4 + piece) & (inner > ROOM))
        batch_of += dot(pick, arrived[:, piece * LANES : (piece + 1) * LANES])
    pre[...] = silu_slope(pre[...])

    for turn in range(4):
        firsts[turn].wait_recv()
        diff = err[turn] + first_in[turn].astype(F32)
        err[turn] = diff
        second_out[turn] = diff.astype(BF16)
        copy = send(
            second_out.at[turn],
            second_in.at[turn],
            sum_s.at[1, turn],
            sum_r.at[1, turn],
            {"mdl": mates[1 - turn % 2]},
        )
        copy.start()
        seconds.append(copy)

    for copy in hists:
        copy.wait_recv()
    counts = jnp.sum(hist_in[...], axis=0)
    share = jnp.where(counts > 0.0, 2.0 / jnp.maximum(counts, 1.0), 0.0)
    weight = jnp.sum(batch_of * share[0:1, :], axis=1, keepdims=True)

    def part_copy(kind, to):
        return send(
            part_out.at[kind, to],
            part_in.at[kind, me_t],
            part_s.at[kind, to],
            part_r.at[kind, me_t],
            {"teach": to},
        )

    per = teachers // 4
    part_rows = part_out.shape[2]
    back = jnp.zeros((used, up.shape[1]), F32)
    for turn in range(4):
        chunk, cols = order[turn]
        seconds[turn].wait_recv()
        total = err[turn] + second_in[turn].astype(F32)
        scaled = (total * weight).astype(BF16)
        grad = dot(scaled, act[...], 0, 0)
        part_out[1, pl.ds(chunk * per, per)] = grad.astype(BF16).reshape(per, part_rows, -1)
        back += dot(scaled, down[cols, :])
        for piece in range(per):
            to = chunk * per + piece

            @pl.when(to != me_t)
            def _():
                part_copy(1, to).start()

    pre_grad = (back * pre[...]).astype(BF16)
    grad = dot(x[...], pre_grad, 0, 0)
    part_out[0] = grad.astype(BF16).reshape(teachers, part_rows, -1)
    for step in steps:
        part_copy(0, peer(step)).start()
    part_in[1, me_t] = part_out[1, me_t]
    part_in[0, me_t] = part_out[0, me_t]

    def part_wait(kind):
        for step in steps:
            source = peer(step)
            send(
                part_out.at[kind, source],
                part_in.at[kind, source],
                part_s.at[kind, source],
                part_r.at[kind, source],
                {"teach": source},
            ).wait_recv()
        return jnp.sum(part_in[kind].astype(F32), axis=0)

    chips = studs // 2
    sum_down = part_wait(1).reshape(chips, part_rows // chips, -1)
    sum_up = part_wait(0).reshape(chips, part_rows // chips, -1)
    last_out[...] = jnp.concatenate([sum_up, sum_down], axis=1).astype(BF16)
    lasts = []
    for step in range(1, studs):
        to = (me_s + step) % studs
        copy = send(
            last_out.at[to // 2],
            last_in.at[me_s],
            last_s.at[step],
            last_r.at[step],
            {"stud": to},
        )
        copy.start()
        lasts.append(copy)
    last_in[me_s] = last_out[me_s // 2]
    for copy in lasts:
        copy.wait_recv()
    total = jnp.sum(last_in[...].astype(F32), axis=0)
    mine = grads.shape[0] // 2
    even = jnp.full((mine, grads.shape[1]), me_s % 2, I32) == 0
    grads[0:mine] = jnp.where(even, total[0:mine], total[mine : 2 * mine])
    grads[mine : 2 * mine] = jnp.where(
        even, total[2 * mine : 3 * mine], total[3 * mine : 4 * mine]
    )

    for copy in going + firsts + hists + seconds + lasts:
        copy.wait_send()
    for step in steps:
        for kind in range(2):
            part_copy(kind, peer(step)).wait_send()


def solution(mesh):
    teachers, studs = mesh.shape["teach"], mesh.shape["stud"]
    side = math.isqrt(teachers)

    def on_device(states, tasks, batches, teach_in, teach_out, up, down):
        width, part = up.shape
        actions = down.shape[0]
        slots, used = teachers * BLOCK, teachers * ROOM
        mine = width // (teachers * studs)
        vmem = pl.BlockSpec(memory_space=pltpu.VMEM)
        dma = pltpu.SemaphoreType.DMA
        hbm = pl.BlockSpec(memory_space=pl.ANY)
        grads = pl.pallas_call(
            functools.partial(kernel, side, teachers, studs),
            out_shape=jax.ShapeDtypeStruct((2 * mine, part), F32),
            in_specs=[hbm, vmem, vmem, hbm, hbm, hbm, hbm],
            out_specs=vmem,
            scratch_shapes=[
                pltpu.VMEM(states.shape, BF16),
                pltpu.VMEM(teach_in.shape, BF16),
                pltpu.VMEM(teach_out.shape, BF16),
                pltpu.VMEM(up.shape, BF16),
                pltpu.VMEM(down.shape, BF16),
                pltpu.VMEM((teachers, BLOCK, width), BF16),
                pltpu.VMEM((teachers, BLOCK, width), BF16),
                pltpu.VMEM((used, width), BF16),
                pltpu.VMEM((used, part), BF16),
                pltpu.VMEM((used, part), BF16),
                pltpu.VMEM((used, part), F32),
                pltpu.VMEM((4, used, actions // 4), F32),
                pltpu.VMEM((4, used, actions // 4), BF16),
                pltpu.VMEM((4, used, actions // 4), BF16),
                pltpu.VMEM((4, used, actions // 4), BF16),
                pltpu.VMEM((4, used, actions // 4), BF16),
                pltpu.VMEM((8, LANES), F32),
                pltpu.VMEM((studs, 8, LANES), F32),
                pltpu.VMEM((2, teachers, width // teachers, part), BF16),
                pltpu.VMEM((2, teachers, width // teachers, part), BF16),
                pltpu.VMEM((studs // 2, 4 * mine, part), BF16),
                pltpu.VMEM((studs, 4 * mine, part), BF16),
                dma((5,)),
                dma((teachers,)),
                dma((teachers,)),
                dma((2, 4)),
                dma((2, 4)),
                dma((studs,)),
                dma((studs,)),
                dma((2, teachers)),
                dma((2, teachers)),
                dma((studs,)),
                dma((studs,)),
            ],
            compiler_params=pltpu.CompilerParams(collective_id=0, has_side_effects=True),
        )(
            states,
            tasks.reshape(1, -1),
            batches.reshape(1, -1),
            teach_in,
            teach_out,
            up,
            down,
        )
        return grads[:mine], grads[mine:]

    in_specs = (
        P(("teach", "stud"), None),
        P(("teach", "stud"), None),
        P(("teach", "stud"), None),
        P("teach", None, "mdl"),
        P("teach", "mdl", None),
        P(None, "mdl"),
        P(None, "mdl"),
    )
    out_specs = (P(("teach", "stud"), "mdl"), P(("teach", "stud"), "mdl"))
    return jax.shard_map(
        on_device, mesh=mesh, in_specs=in_specs, out_specs=out_specs, check_vma=False
    )
```

```python
import functools
import math

import jax
import jax.numpy as jnp
from jax import lax
from jax.experimental import pallas as pl
from jax.experimental.pallas import tpu as pltpu
from jax.sharding import PartitionSpec as P

MESH = pl.DeviceIdType.MESH
F32, BF16, I32 = jnp.float32, jnp.bfloat16, jnp.int32
ROOM = 12
BLOCK = 16
LANES = 128
PARTS = 4


def dot(a, b, ca=1, cb=0):
    return lax.dot_general(a, b, (((ca,), (cb,)), ((), ())), preferred_element_type=F32)


def iota(shape, dim):
    return lax.broadcasted_iota(I32, shape, dim)


def onehot(mask):
    return jnp.where(mask, 1.0, 0.0).astype(BF16)


def silu(value):
    return value * jax.nn.sigmoid(value)


def silu_slope(value):
    sig = jax.nn.sigmoid(value)
    return sig * (1.0 + value * (1.0 - sig))


def kernel(
    side,
    teachers,
    studs,
    states_hbm,
    tasks_hbm,
    batches_hbm,
    teach_in_hbm,
    teach_out_hbm,
    up_hbm,
    down_hbm,
    grads,
    tasks,
    batches,
    states,
    teach_in,
    teach_out,
    up,
    down,
    out,
    got,
    x,
    hid,
    act,
    pre,
    err,
    first_out,
    first_in,
    second_out,
    second_in,
    scaled_mid,
    scaled_end,
    weight,
    hist_out,
    hist_in,
    part_out,
    part_in,
    last_out,
    last_in,
    load_s,
    go_s,
    go_r,
    sum_s,
    sum_r,
    hist_s,
    hist_r,
    part_s,
    part_r,
    last_s,
    last_r,
):
    me_t, me_s, me_m = lax.axis_index("teach"), lax.axis_index("stud"), lax.axis_index("mdl")
    my_x, my_y = me_t // side, me_t % side
    rows, width = states.shape
    slots, used = teachers * BLOCK, teachers * ROOM
    pieces = width // LANES
    mates = ((me_m + 1) % 4, (me_m + 3) % 4)

    def hops(step):
        dx, dy = step // side, step % side
        return min(dx, side - dx) + min(dy, side - dy)

    steps = sorted(range(1, teachers), key=lambda step: -hops(step))

    def peer(step):
        return ((my_x + step // side) % side) * side + (my_y + step % side) % side

    barrier = pltpu.get_barrier_semaphore()
    for step in steps:
        pl.semaphore_signal(barrier, inc=1, device_id={"teach": peer(step)}, device_id_type=MESH)
    for step in range(1, studs):
        pl.semaphore_signal(
            barrier, inc=1, device_id={"stud": (me_s + step) % studs}, device_id_type=MESH
        )
    for mate in mates:
        pl.semaphore_signal(barrier, inc=1, device_id={"mdl": mate}, device_id_type=MESH)

    def send(src, dst, send_sem, recv_sem, where):
        copy = pltpu.make_async_remote_copy(
            src_ref=src,
            dst_ref=dst,
            send_sem=send_sem,
            recv_sem=recv_sem,
            device_id=where,
            device_id_type=MESH,
        )
        return copy

    loads = []
    for index, (source, held) in enumerate(
        (
            (tasks_hbm, tasks),
            (batches_hbm, batches),
            (states_hbm, states),
            (teach_in_hbm, teach_in),
            (up_hbm, up),
            (down_hbm, down),
            (teach_out_hbm, teach_out),
        )
    ):
        loads.append(pltpu.make_async_copy(source, held, load_s.at[index]))
        loads[-1].start()

    earlier = onehot(iota((rows, rows), 0) < iota((rows, rows), 1))
    place = iota((slots, rows), 0)
    for load in loads[:2]:
        load.wait()

    hot = jnp.where(tasks[...] == iota((teachers, rows), 0), 1.0, 0.0)
    before = jnp.sum(dot(hot.astype(BF16), earlier) * hot, axis=0, keepdims=True)
    slot = tasks[...] * BLOCK + before.astype(I32)
    note = ((slot >> 4) * BLOCK + ROOM + 1 + ((slot & 15) >> 2)) * 4 + (slot & 3)
    batch_hot = onehot(batches[...] == iota((LANES, rows), 0))
    dispatch = onehot(place == slot)
    loads[2].wait()
    for piece in range(pieces):
        noted = place * 4 + piece == note
        if piece == 0:
            noted = noted | ((place & 15) == ROOM)
        cols = slice(piece * LANES, (piece + 1) * LANES)
        block = dot(dispatch, states[:, cols]) + dot(onehot(noted), batch_hot, 1, 1)
        out[:, :, cols] = block.astype(BF16).reshape(teachers, BLOCK, LANES)

    pl.semaphore_wait(barrier, teachers - 1 + studs - 1 + 2)

    going = []
    for step in steps:
        to = peer(step)
        copy = send(
            out.at[to], got.at[me_t], go_s.at[step], go_r.at[step], {"teach": to}
        )
        copy.start()
        going.append(copy)
    got[me_t] = out[me_t]

    source = iota((used, slots), 1)
    target = iota((used, slots), 0)
    base, inner = (source >> 4) * ROOM, source & 15
    keep = onehot((target == base + inner) & (inner < ROOM))

    for copy in going:
        copy.wait_recv()

    arrived = got[...].reshape(slots, width)

    for load in loads[3:]:
        load.wait()
    x[...] = dot(keep, arrived).astype(BF16)
    marks = onehot((iota((8, slots), 1) & 15) == ROOM)
    hist_out[...] = dot(marks, arrived[:, :LANES])
    hists = []
    for step in range(1, studs):
        to = (me_s + step) % studs
        copy = send(
            hist_out, hist_in.at[me_s], hist_s.at[step], hist_r.at[step], {"stud": to}
        )
        copy.start()
        hists.append(copy)
    hist_in[me_s] = hist_out[...]

    hid[...] = silu(dot(x[...], teach_in[0])).astype(BF16)
    pre[...] = dot(x[...], up[...])
    act[...] = silu(pre[...]).astype(BF16)

    chunks, spans = [], []
    for role in range(4):
        chunks.append((me_m + 4 - role + my_x * 4 // side) % 4)
        spans.append(pl.ds(pl.multiple_of(chunks[role] * LANES, LANES), LANES))

    def diff(role):
        cols = spans[role]
        return dot(act[...], down[cols, :], 1, 1) - dot(hid[...], teach_out[0, :, cols])

    parts = [slice(part * used // PARTS, (part + 1) * used // PARTS) for part in range(PARTS)]
    firsts, seconds, thirds = [], [], []
    for side_of, role in enumerate((0, 3)):
        first_out[side_of] = diff(role).astype(BF16)
    for part, at in enumerate(parts):
        for side_of in range(2):
            copy = send(
                first_out.at[side_of, at],
                first_in.at[side_of, at],
                sum_s.at[0, side_of, part],
                sum_r.at[0, side_of, part],
                {"mdl": mates[side_of]},
            )
            copy.start()
            firsts.append(copy)
    for side_of, role in enumerate((1, 2)):
        err[side_of] = diff(role)

    batch_of = jnp.zeros((used, LANES), F32)
    for piece in range(pieces):
        pick = onehot((target == base + (inner - ROOM - 1) * 4 + piece) & (inner > ROOM))
        batch_of += dot(pick, arrived[:, piece * LANES : (piece + 1) * LANES])
    pre[...] = silu_slope(pre[...])

    for part, at in enumerate(parts):
        for side_of in range(2):
            firsts[part * 2 + side_of].wait_recv()
            total = err[side_of, at] + first_in[side_of, at].astype(F32)
            err[side_of, at] = total
            second_out[side_of, at] = total.astype(BF16)
            copy = send(
                second_out.at[side_of, at],
                second_in.at[1 - side_of, at],
                sum_s.at[1, side_of, part],
                sum_r.at[1, 1 - side_of, part],
                {"mdl": mates[side_of]},
            )
            copy.start()
            seconds.append(copy)

    for copy in hists:
        copy.wait_recv()
    counts = jnp.sum(hist_in[...], axis=0)
    share = jnp.where(counts > 0.0, 2.0 / jnp.maximum(counts, 1.0), 0.0)
    weight[...] = jnp.broadcast_to(
        jnp.sum(batch_of * share[0:1, :], axis=1, keepdims=True), weight.shape
    )

    for part, at in enumerate(parts):
        for side_of in range(2):
            seconds[part * 2 + 1 - side_of].wait_recv()
            total = err[side_of, at] + second_in[side_of, at].astype(F32)
            scaled_mid[side_of, at] = (total * weight[at]).astype(BF16)
            copy = send(
                scaled_mid.at[side_of, at],
                scaled_end.at[side_of, at],
                sum_s.at[2, side_of, part],
                sum_r.at[2, side_of, part],
                {"mdl": mates[1 - side_of]},
            )
            copy.start()
            thirds.append(copy)

    def part_copy(kind, to):
        return send(
            part_out.at[kind, to],
            part_in.at[kind, me_t],
            part_s.at[kind, to],
            part_r.at[kind, me_t],
            {"teach": to},
        )

    per = teachers // 4
    part_rows = part_out.shape[2]
    back = jnp.zeros((used, up.shape[1]), F32)
    for turn, role in enumerate((1, 2, 0, 3)):
        chunk, cols, side_of = chunks[role], spans[role], turn % 2
        if turn < 2:
            scaled = scaled_mid[side_of]
        else:
            for part in range(PARTS):
                thirds[part * 2 + side_of].wait_recv()
            scaled = scaled_end[side_of]
        grad = dot(scaled, act[...], 0, 0)
        part_out[1, pl.ds(chunk * per, per)] = grad.astype(BF16).reshape(per, part_rows, -1)
        back += dot(scaled, down[cols, :])
        for piece in range(per):
            to = chunk * per + piece

            @pl.when(to != me_t)
            def _():
                part_copy(1, to).start()

    pre_grad = (back * pre[...]).astype(BF16)
    grad = dot(x[...], pre_grad, 0, 0)
    part_out[0] = grad.astype(BF16).reshape(teachers, part_rows, -1)
    for step in steps:
        part_copy(0, peer(step)).start()
    part_in[1, me_t] = part_out[1, me_t]
    part_in[0, me_t] = part_out[0, me_t]

    def part_wait(kind):
        for step in steps:
            source = peer(step)
            send(
                part_out.at[kind, source],
                part_in.at[kind, source],
                part_s.at[kind, source],
                part_r.at[kind, source],
                {"teach": source},
            ).wait_recv()
        return jnp.sum(part_in[kind].astype(F32), axis=0)

    chips = studs // 2
    sum_down = part_wait(1).reshape(chips, part_rows // chips, -1)
    sum_up = part_wait(0).reshape(chips, part_rows // chips, -1)
    last_out[...] = jnp.concatenate([sum_up, sum_down], axis=1).astype(BF16)
    lasts = []
    for step in range(1, studs):
        to = (me_s + step) % studs
        copy = send(
            last_out.at[to // 2],
            last_in.at[me_s],
            last_s.at[step],
            last_r.at[step],
            {"stud": to},
        )
        copy.start()
        lasts.append(copy)
    last_in[me_s] = last_out[me_s // 2]
    for copy in lasts:
        copy.wait_recv()
    total = jnp.sum(last_in[...].astype(F32), axis=0)
    mine = grads.shape[0] // 2
    even = jnp.full((mine, grads.shape[1]), me_s % 2, I32) == 0
    grads[0:mine] = jnp.where(even, total[0:mine], total[mine : 2 * mine])
    grads[mine : 2 * mine] = jnp.where(
        even, total[2 * mine : 3 * mine], total[3 * mine : 4 * mine]
    )

    for copy in going + hists + firsts + seconds + thirds + lasts:
        copy.wait_send()
    for step in steps:
        for kind in range(2):
            part_copy(kind, peer(step)).wait_send()


def solution(mesh):
    teachers, studs = mesh.shape["teach"], mesh.shape["stud"]
    side = math.isqrt(teachers)

    def on_device(states, tasks, batches, teach_in, teach_out, up, down):
        width, part = up.shape
        actions = down.shape[0]
        slots, used = teachers * BLOCK, teachers * ROOM
        mine = width // (teachers * studs)
        vmem = pl.BlockSpec(memory_space=pltpu.VMEM)
        dma = pltpu.SemaphoreType.DMA
        hbm = pl.BlockSpec(memory_space=pl.ANY)
        grads = pl.pallas_call(
            functools.partial(kernel, side, teachers, studs),
            out_shape=jax.ShapeDtypeStruct((2 * mine, part), F32),
            in_specs=[hbm] * 7,
            out_specs=vmem,
            scratch_shapes=[
                pltpu.VMEM((1, states.shape[0]), I32),
                pltpu.VMEM((1, states.shape[0]), I32),
                pltpu.VMEM(states.shape, BF16),
                pltpu.VMEM(teach_in.shape, BF16),
                pltpu.VMEM(teach_out.shape, BF16),
                pltpu.VMEM(up.shape, BF16),
                pltpu.VMEM(down.shape, BF16),
                pltpu.VMEM((teachers, BLOCK, width), BF16),
                pltpu.VMEM((teachers, BLOCK, width), BF16),
                pltpu.VMEM((used, width), BF16),
                pltpu.VMEM((used, part), BF16),
                pltpu.VMEM((used, part), BF16),
                pltpu.VMEM((used, part), F32),
                pltpu.VMEM((2, used, actions // 4), F32),
                pltpu.VMEM((2, used, actions // 4), BF16),
                pltpu.VMEM((2, used, actions // 4), BF16),
                pltpu.VMEM((2, used, actions // 4), BF16),
                pltpu.VMEM((2, used, actions // 4), BF16),
                pltpu.VMEM((2, used, actions // 4), BF16),
                pltpu.VMEM((2, used, actions // 4), BF16),
                pltpu.VMEM((used, LANES), F32),
                pltpu.VMEM((8, LANES), F32),
                pltpu.VMEM((studs, 8, LANES), F32),
                pltpu.VMEM((2, teachers, width // teachers, part), BF16),
                pltpu.VMEM((2, teachers, width // teachers, part), BF16),
                pltpu.VMEM((studs // 2, 4 * mine, part), BF16),
                pltpu.VMEM((studs, 4 * mine, part), BF16),
                dma((7,)),
                dma((teachers,)),
                dma((teachers,)),
                dma((3, 2, PARTS)),
                dma((3, 2, PARTS)),
                dma((studs,)),
                dma((studs,)),
                dma((2, teachers)),
                dma((2, teachers)),
                dma((studs,)),
                dma((studs,)),
            ],
            compiler_params=pltpu.CompilerParams(collective_id=0, has_side_effects=True),
        )(
            states,
            tasks.reshape(1, -1),
            batches.reshape(1, -1),
            teach_in,
            teach_out,
            up,
            down,
        )
        return grads[:mine], grads[mine:]

    in_specs = (
        P(("teach", "stud"), None),
        P(("teach", "stud"), None),
        P(("teach", "stud"), None),
        P("teach", None, "mdl"),
        P("teach", "mdl", None),
        P(None, "mdl"),
        P(None, "mdl"),
    )
    out_specs = (P(("teach", "stud"), "mdl"), P(("teach", "stud"), "mdl"))
    return jax.shard_map(
        on_device, mesh=mesh, in_specs=in_specs, out_specs=out_specs, check_vma=False
    )
```

```python
import functools
import math

import jax
import jax.numpy as jnp
from jax import lax
from jax.experimental import pallas as pl
from jax.experimental.pallas import tpu as pltpu
from jax.sharding import PartitionSpec as P

MESH = pl.DeviceIdType.MESH
F32, BF16, I32 = jnp.float32, jnp.bfloat16, jnp.int32
ROOM = 12
BLOCK = 16
LANES = 128
PARTS = 4


def dot(a, b, ca=1, cb=0):
    return lax.dot_general(a, b, (((ca,), (cb,)), ((), ())), preferred_element_type=F32)


def iota(shape, dim):
    return lax.broadcasted_iota(I32, shape, dim)


def onehot(mask):
    return jnp.where(mask, 1.0, 0.0).astype(BF16)


def silu(value):
    return value * jax.nn.sigmoid(value)


def silu_slope(value):
    sig = jax.nn.sigmoid(value)
    return sig * (1.0 + value * (1.0 - sig))


def kernel(
    side,
    teachers,
    studs,
    states_hbm,
    tasks_hbm,
    batches_hbm,
    teach_in_hbm,
    teach_out_hbm,
    up_hbm,
    down_hbm,
    grads,
    tasks,
    batches,
    states,
    teach_in,
    teach_out,
    up,
    down,
    out,
    got,
    x,
    hid,
    act,
    pre,
    err,
    first_out,
    first_in,
    second_out,
    second_in,
    scaled_mid,
    scaled_end,
    weight,
    hist_out,
    hist_in,
    part_out,
    part_in,
    last_out,
    last_in,
    load_s,
    go_s,
    go_r,
    sum_s,
    sum_r,
    hist_s,
    hist_r,
    part_s,
    part_r,
    last_s,
    last_r,
):
    me_t, me_s, me_m = lax.axis_index("teach"), lax.axis_index("stud"), lax.axis_index("mdl")
    my_x, my_y = me_t // side, me_t % side
    rows, width = states.shape
    slots, used = teachers * BLOCK, teachers * ROOM
    pieces = width // LANES
    mates = ((me_m + 1) % 4, (me_m + 3) % 4)

    def hops(step):
        dx, dy = step // side, step % side
        return min(dx, side - dx) + min(dy, side - dy)

    steps = sorted(range(1, teachers), key=lambda step: -hops(step))

    def peer(step):
        return ((my_x + step // side) % side) * side + (my_y + step % side) % side

    barrier = pltpu.get_barrier_semaphore()
    for step in steps:
        pl.semaphore_signal(barrier, inc=1, device_id={"teach": peer(step)}, device_id_type=MESH)
    for step in range(1, studs):
        pl.semaphore_signal(
            barrier, inc=1, device_id={"stud": (me_s + step) % studs}, device_id_type=MESH
        )
    for mate in mates:
        pl.semaphore_signal(barrier, inc=1, device_id={"mdl": mate}, device_id_type=MESH)

    def send(src, dst, send_sem, recv_sem, where):
        copy = pltpu.make_async_remote_copy(
            src_ref=src,
            dst_ref=dst,
            send_sem=send_sem,
            recv_sem=recv_sem,
            device_id=where,
            device_id_type=MESH,
        )
        return copy

    loads = []
    for index, (source, held) in enumerate(
        (
            (tasks_hbm, tasks),
            (batches_hbm, batches),
            (states_hbm, states),
            (teach_in_hbm, teach_in),
            (up_hbm, up),
            (down_hbm, down),
            (teach_out_hbm, teach_out),
        )
    ):
        loads.append(pltpu.make_async_copy(source, held, load_s.at[index]))
    for load in loads[:3]:
        load.start()

    earlier = onehot(iota((rows, rows), 0) < iota((rows, rows), 1))
    place = iota((slots, rows), 0)
    for load in loads[:2]:
        load.wait()

    hot = jnp.where(tasks[...] == iota((teachers, rows), 0), 1.0, 0.0)
    before = jnp.sum(dot(hot.astype(BF16), earlier) * hot, axis=0, keepdims=True)
    slot = tasks[...] * BLOCK + before.astype(I32)
    note = ((slot >> 4) * BLOCK + ROOM + 1 + ((slot & 15) >> 2)) * 4 + (slot & 3)
    batch_hot = onehot(batches[...] == iota((LANES, rows), 0))
    dispatch = onehot(place == slot)
    loads[2].wait()
    for load in loads[3:]:
        load.start()
    for piece in range(pieces):
        noted = place * 4 + piece == note
        if piece == 0:
            noted = noted | ((place & 15) == ROOM)
        cols = slice(piece * LANES, (piece + 1) * LANES)
        block = dot(dispatch, states[:, cols]) + dot(onehot(noted), batch_hot, 1, 1)
        out[:, :, cols] = block.astype(BF16).reshape(teachers, BLOCK, LANES)

    pl.semaphore_wait(barrier, teachers - 1 + studs - 1 + 2)

    going = []
    for step in steps:
        to = peer(step)
        copy = send(
            out.at[to], got.at[me_t], go_s.at[step], go_r.at[step], {"teach": to}
        )
        copy.start()
        going.append(copy)
    got[me_t] = out[me_t]

    source = iota((used, slots), 1)
    target = iota((used, slots), 0)
    base, inner = (source >> 4) * ROOM, source & 15
    keep = onehot((target == base + inner) & (inner < ROOM))

    for copy in going:
        copy.wait_recv()

    arrived = got[...].reshape(slots, width)

    for load in loads[3:]:
        load.wait()
    x[...] = dot(keep, arrived).astype(BF16)
    hid[...] = silu(dot(x[...], teach_in[0])).astype(BF16)
    pre[...] = dot(x[...], up[...])
    act[...] = silu(pre[...]).astype(BF16)

    chunks, spans = [], []
    for role in range(4):
        chunks.append((me_m + 4 - role + my_x * 4 // side) % 4)
        spans.append(pl.ds(pl.multiple_of(chunks[role] * LANES, LANES), LANES))

    def diff(role):
        cols = spans[role]
        return dot(act[...], down[cols, :], 1, 1) - dot(hid[...], teach_out[0, :, cols])

    parts = [slice(part * used // PARTS, (part + 1) * used // PARTS) for part in range(PARTS)]
    firsts, seconds, thirds = [], [], []
    for side_of, role in enumerate((0, 3)):
        first_out[side_of] = diff(role).astype(BF16)
    for part, at in enumerate(parts):
        for side_of in range(2):
            copy = send(
                first_out.at[side_of, at],
                first_in.at[side_of, at],
                sum_s.at[0, side_of, part],
                sum_r.at[0, side_of, part],
                {"mdl": mates[side_of]},
            )
            copy.start()
            firsts.append(copy)
    for side_of, role in enumerate((1, 2)):
        err[side_of] = diff(role)

    marks = onehot((iota((8, slots), 1) & 15) == ROOM)
    hist_out[...] = dot(marks, arrived[:, :LANES])
    hists = []
    for step in range(1, studs):
        to = (me_s + step) % studs
        copy = send(
            hist_out, hist_in.at[me_s], hist_s.at[step], hist_r.at[step], {"stud": to}
        )
        copy.start()
        hists.append(copy)
    hist_in[me_s] = hist_out[...]

    batch_of = jnp.zeros((used, LANES), F32)
    for piece in range(pieces):
        pick = onehot((target == base + (inner - ROOM - 1) * 4 + piece) & (inner > ROOM))
        batch_of += dot(pick, arrived[:, piece * LANES : (piece + 1) * LANES])
    pre[...] = silu_slope(pre[...])

    for part, at in enumerate(parts):
        for side_of in range(2):
            firsts[part * 2 + side_of].wait_recv()
            total = err[side_of, at] + first_in[side_of, at].astype(F32)
            err[side_of, at] = total
            second_out[side_of, at] = total.astype(BF16)
            copy = send(
                second_out.at[side_of, at],
                second_in.at[1 - side_of, at],
                sum_s.at[1, side_of, part],
                sum_r.at[1, 1 - side_of, part],
                {"mdl": mates[side_of]},
            )
            copy.start()
            seconds.append(copy)

    for copy in hists:
        copy.wait_recv()
    counts = jnp.sum(hist_in[...], axis=0)
    share = jnp.where(counts > 0.0, 2.0 / jnp.maximum(counts, 1.0), 0.0)
    weight[...] = jnp.broadcast_to(
        jnp.sum(batch_of * share[0:1, :], axis=1, keepdims=True), weight.shape
    )

    for part, at in enumerate(parts):
        for side_of in range(2):
            seconds[part * 2 + 1 - side_of].wait_recv()
            total = err[side_of, at] + second_in[side_of, at].astype(F32)
            scaled_mid[side_of, at] = (total * weight[at]).astype(BF16)
            copy = send(
                scaled_mid.at[side_of, at],
                scaled_end.at[side_of, at],
                sum_s.at[2, side_of, part],
                sum_r.at[2, side_of, part],
                {"mdl": mates[1 - side_of]},
            )
            copy.start()
            thirds.append(copy)

    def part_copy(kind, to):
        return send(
            part_out.at[kind, to],
            part_in.at[kind, me_t],
            part_s.at[kind, to],
            part_r.at[kind, me_t],
            {"teach": to},
        )

    per = teachers // 4
    part_rows = part_out.shape[2]
    back = jnp.zeros((used, up.shape[1]), F32)
    for turn, role in enumerate((1, 2, 0, 3)):
        chunk, cols, side_of = chunks[role], spans[role], turn % 2
        if turn < 2:
            scaled = scaled_mid[side_of]
        else:
            for part in range(PARTS):
                thirds[part * 2 + side_of].wait_recv()
            scaled = scaled_end[side_of]
        grad = dot(scaled, act[...], 0, 0)
        part_out[1, pl.ds(chunk * per, per)] = grad.astype(BF16).reshape(per, part_rows, -1)
        back += dot(scaled, down[cols, :])
        for piece in range(per):
            to = chunk * per + piece

            @pl.when(to != me_t)
            def _():
                part_copy(1, to).start()

    pre_grad = (back * pre[...]).astype(BF16)
    for turn in (2, 1, 3, 0):
        block = (my_x + turn * side // 4) % 4
        cols = pl.ds(pl.multiple_of(block * LANES, LANES), LANES)
        grad = dot(x[:, cols], pre_grad, 0, 0)
        part_out[0, pl.ds(block * per, per)] = grad.astype(BF16).reshape(per, part_rows, -1)
        for piece in range(per):
            to = block * per + (my_y + piece) % per

            @pl.when(to != me_t)
            def _():
                part_copy(0, to).start()

    part_in[1, me_t] = part_out[1, me_t]
    part_in[0, me_t] = part_out[0, me_t]

    def part_wait(kind):
        for step in steps:
            source = peer(step)
            send(
                part_out.at[kind, source],
                part_in.at[kind, source],
                part_s.at[kind, source],
                part_r.at[kind, source],
                {"teach": source},
            ).wait_recv()
        return jnp.sum(part_in[kind].astype(F32), axis=0)

    chips = studs // 2
    sum_down = part_wait(1).reshape(chips, part_rows // chips, -1)
    sum_up = part_wait(0).reshape(chips, part_rows // chips, -1)
    last_out[...] = jnp.concatenate([sum_up, sum_down], axis=1).astype(BF16)
    lasts = []
    for step in range(1, studs):
        to = (me_s + step) % studs
        copy = send(
            last_out.at[to // 2],
            last_in.at[me_s],
            last_s.at[step],
            last_r.at[step],
            {"stud": to},
        )
        copy.start()
        lasts.append(copy)
    last_in[me_s] = last_out[me_s // 2]
    for copy in lasts:
        copy.wait_recv()
    total = jnp.sum(last_in[...].astype(F32), axis=0)
    mine = grads.shape[0] // 2
    even = jnp.full((mine, grads.shape[1]), me_s % 2, I32) == 0
    grads[0:mine] = jnp.where(even, total[0:mine], total[mine : 2 * mine])
    grads[mine : 2 * mine] = jnp.where(
        even, total[2 * mine : 3 * mine], total[3 * mine : 4 * mine]
    )

    for copy in going + hists + firsts + seconds + thirds + lasts:
        copy.wait_send()
    for step in steps:
        for kind in range(2):
            part_copy(kind, peer(step)).wait_send()


def solution(mesh):
    teachers, studs = mesh.shape["teach"], mesh.shape["stud"]
    side = math.isqrt(teachers)

    def on_device(states, tasks, batches, teach_in, teach_out, up, down):
        width, part = up.shape
        actions = down.shape[0]
        slots, used = teachers * BLOCK, teachers * ROOM
        mine = width // (teachers * studs)
        vmem = pl.BlockSpec(memory_space=pltpu.VMEM)
        dma = pltpu.SemaphoreType.DMA
        hbm = pl.BlockSpec(memory_space=pl.ANY)
        grads = pl.pallas_call(
            functools.partial(kernel, side, teachers, studs),
            out_shape=pltpu.VMEM((2 * mine, part), F32),
            in_specs=[hbm] * 7,
            out_specs=vmem,
            scratch_shapes=[
                pltpu.VMEM((1, states.shape[0]), I32),
                pltpu.VMEM((1, states.shape[0]), I32),
                pltpu.VMEM(states.shape, BF16),
                pltpu.VMEM(teach_in.shape, BF16),
                pltpu.VMEM(teach_out.shape, BF16),
                pltpu.VMEM(up.shape, BF16),
                pltpu.VMEM(down.shape, BF16),
                pltpu.VMEM((teachers, BLOCK, width), BF16),
                pltpu.VMEM((teachers, BLOCK, width), BF16),
                pltpu.VMEM((used, width), BF16),
                pltpu.VMEM((used, part), BF16),
                pltpu.VMEM((used, part), BF16),
                pltpu.VMEM((used, part), F32),
                pltpu.VMEM((2, used, actions // 4), F32),
                pltpu.VMEM((2, used, actions // 4), BF16),
                pltpu.VMEM((2, used, actions // 4), BF16),
                pltpu.VMEM((2, used, actions // 4), BF16),
                pltpu.VMEM((2, used, actions // 4), BF16),
                pltpu.VMEM((2, used, actions // 4), BF16),
                pltpu.VMEM((2, used, actions // 4), BF16),
                pltpu.VMEM((used, LANES), F32),
                pltpu.VMEM((8, LANES), F32),
                pltpu.VMEM((studs, 8, LANES), F32),
                pltpu.VMEM((2, teachers, width // teachers, part), BF16),
                pltpu.VMEM((2, teachers, width // teachers, part), BF16),
                pltpu.VMEM((studs // 2, 4 * mine, part), BF16),
                pltpu.VMEM((studs, 4 * mine, part), BF16),
                dma((7,)),
                dma((teachers,)),
                dma((teachers,)),
                dma((3, 2, PARTS)),
                dma((3, 2, PARTS)),
                dma((studs,)),
                dma((studs,)),
                dma((2, teachers)),
                dma((2, teachers)),
                dma((studs,)),
                dma((studs,)),
            ],
            compiler_params=pltpu.CompilerParams(collective_id=0, has_side_effects=True),
        )(
            states,
            tasks.reshape(1, -1),
            batches.reshape(1, -1),
            teach_in,
            teach_out,
            up,
            down,
        )
        return grads[:mine], grads[mine:]

    in_specs = (
        P(("teach", "stud"), None),
        P(("teach", "stud"), None),
        P(("teach", "stud"), None),
        P("teach", None, "mdl"),
        P("teach", "mdl", None),
        P(None, "mdl"),
        P(None, "mdl"),
    )
    out_specs = (P(("teach", "stud"), "mdl"), P(("teach", "stud"), "mdl"))
    return jax.shard_map(
        on_device, mesh=mesh, in_specs=in_specs, out_specs=out_specs, check_vma=False
    )
```

```python
import functools
import math

import jax
import jax.numpy as jnp
from jax import lax
from jax.experimental import pallas as pl
from jax.experimental.pallas import tpu as pltpu
from jax.sharding import PartitionSpec as P

MESH = pl.DeviceIdType.MESH
F32, BF16, I32 = jnp.float32, jnp.bfloat16, jnp.int32
ROOM = 12
BLOCK = 16
LANES = 128
PARTS = 4


def dot(a, b, ca=1, cb=0):
    return lax.dot_general(a, b, (((ca,), (cb,)), ((), ())), preferred_element_type=F32)


def iota(shape, dim):
    return lax.broadcasted_iota(I32, shape, dim)


def onehot(mask):
    return jnp.where(mask, 1.0, 0.0).astype(BF16)


def silu(value):
    return value * jax.nn.sigmoid(value)


def silu_slope(value):
    sig = jax.nn.sigmoid(value)
    return sig * (1.0 + value * (1.0 - sig))


def kernel(
    side,
    teachers,
    studs,
    states_hbm,
    tasks_hbm,
    batches_hbm,
    teach_in_hbm,
    teach_out_hbm,
    up_hbm,
    down_hbm,
    grads,
    tasks,
    batches,
    states,
    teach_in,
    teach_out,
    up,
    down,
    out,
    got,
    x,
    hid,
    act,
    pre,
    err,
    first_out,
    first_in,
    second_out,
    second_in,
    scaled_mid,
    scaled_end,
    weight,
    hist_out,
    hist_in,
    sums_out,
    sums_in,
    part_out,
    part_in,
    last_out,
    last_in,
    load_s,
    go_s,
    go_r,
    sum_s,
    sum_r,
    hist_s,
    hist_r,
    sums_s,
    sums_r,
    part_s,
    part_r,
    last_s,
    last_r,
):
    me_t, me_s, me_m = lax.axis_index("teach"), lax.axis_index("stud"), lax.axis_index("mdl")
    my_x, my_y = me_t // side, me_t % side
    rows, width = states.shape
    slots, used = teachers * BLOCK, teachers * ROOM
    pieces = width // LANES
    mates = ((me_m + 1) % 4, (me_m + 3) % 4)

    def hops(step):
        dx, dy = step // side, step % side
        return min(dx, side - dx) + min(dy, side - dy)

    steps = sorted(range(1, teachers), key=lambda step: -hops(step))

    def peer(step):
        return ((my_x + step // side) % side) * side + (my_y + step % side) % side

    barrier = pltpu.get_barrier_semaphore()
    for step in steps:
        pl.semaphore_signal(barrier, inc=1, device_id={"teach": peer(step)}, device_id_type=MESH)
    for step in range(1, studs):
        pl.semaphore_signal(
            barrier, inc=1, device_id={"stud": (me_s + step) % studs}, device_id_type=MESH
        )
    for mate in mates:
        pl.semaphore_signal(barrier, inc=1, device_id={"mdl": mate}, device_id_type=MESH)

    def send(src, dst, send_sem, recv_sem, where):
        copy = pltpu.make_async_remote_copy(
            src_ref=src,
            dst_ref=dst,
            send_sem=send_sem,
            recv_sem=recv_sem,
            device_id=where,
            device_id_type=MESH,
        )
        return copy

    loads = []
    for index, (source, held) in enumerate(
        (
            (tasks_hbm, tasks),
            (batches_hbm, batches),
            (states_hbm, states),
            (teach_in_hbm, teach_in),
            (up_hbm, up),
            (down_hbm, down),
            (teach_out_hbm, teach_out),
        )
    ):
        loads.append(pltpu.make_async_copy(source, held, load_s.at[index]))
    for load in loads[:3]:
        load.start()

    earlier = onehot(iota((rows, rows), 0) < iota((rows, rows), 1))
    place = iota((slots, rows), 0)
    for load in loads[:2]:
        load.wait()

    hot = jnp.where(tasks[...] == iota((teachers, rows), 0), 1.0, 0.0)
    before = jnp.sum(dot(hot.astype(BF16), earlier) * hot, axis=0, keepdims=True)
    slot = tasks[...] * BLOCK + before.astype(I32)
    note = ((slot >> 4) * BLOCK + ROOM + 1 + ((slot & 15) >> 2)) * 4 + (slot & 3)
    batch_hot = onehot(batches[...] == iota((LANES, rows), 0))
    hist_out[...] = dot(jnp.ones((8, rows), BF16), batch_hot, 1, 1)
    dispatch = onehot(place == slot)
    loads[2].wait()
    for load in loads[3:]:
        load.start()
    for piece in range(pieces):
        noted = place * 4 + piece == note
        cols = slice(piece * LANES, (piece + 1) * LANES)
        block = dot(dispatch, states[:, cols]) + dot(onehot(noted), batch_hot, 1, 1)
        out[:, :, cols] = block.astype(BF16).reshape(teachers, BLOCK, LANES)

    pl.semaphore_wait(barrier, teachers - 1 + studs - 1 + 2)

    going = []
    for step in steps:
        to = peer(step)
        copy = send(
            out.at[to], got.at[me_t], go_s.at[step], go_r.at[step], {"teach": to}
        )
        copy.start()
        going.append(copy)
    got[me_t] = out[me_t]
    hists = []
    for step in range(1, studs):
        to = (me_s + step) % studs
        copy = send(
            hist_out, hist_in.at[me_s], hist_s.at[step], hist_r.at[step], {"stud": to}
        )
        copy.start()
        hists.append(copy)
    hist_in[me_s] = hist_out[...]

    source = iota((used, slots), 1)
    target = iota((used, slots), 0)
    base, inner = (source >> 4) * ROOM, source & 15
    keep = onehot((target == base + inner) & (inner < ROOM))

    for copy in going:
        copy.wait_recv()

    arrived = got[...].reshape(slots, width)

    for load in loads[3:]:
        load.wait()
    x[...] = dot(keep, arrived).astype(BF16)
    hid[...] = silu(dot(x[...], teach_in[0])).astype(BF16)
    pre[...] = dot(x[...], up[...])
    act[...] = silu(pre[...]).astype(BF16)

    chunks, spans = [], []
    for role in range(4):
        chunks.append((me_m + 4 - role + my_x * 4 // side) % 4)
        spans.append(pl.ds(pl.multiple_of(chunks[role] * LANES, LANES), LANES))

    def diff(role):
        cols = spans[role]
        return dot(act[...], down[cols, :], 1, 1) - dot(hid[...], teach_out[0, :, cols])

    parts = [slice(part * used // PARTS, (part + 1) * used // PARTS) for part in range(PARTS)]
    firsts, seconds, thirds = [], [], []
    for side_of, role in enumerate((0, 3)):
        first_out[side_of] = diff(role).astype(BF16)
    for part, at in enumerate(parts):
        for side_of in range(2):
            copy = send(
                first_out.at[side_of, at],
                first_in.at[side_of, at],
                sum_s.at[0, side_of, part],
                sum_r.at[0, side_of, part],
                {"mdl": mates[side_of]},
            )
            copy.start()
            firsts.append(copy)
    for side_of, role in enumerate((1, 2)):
        err[side_of] = diff(role)

    for copy in hists:
        copy.wait_recv()
    sums_out[...] = jnp.sum(hist_in[...], axis=0)
    sums = []
    for step in steps:
        copy = send(
            sums_out, sums_in.at[me_t], sums_s.at[step], sums_r.at[step], {"teach": peer(step)}
        )
        copy.start()
        sums.append(copy)
    sums_in[me_t] = sums_out[...]
    batch_of = jnp.zeros((used, LANES), F32)
    for piece in range(pieces):
        pick = onehot((target == base + (inner - ROOM - 1) * 4 + piece) & (inner > ROOM))
        batch_of += dot(pick, arrived[:, piece * LANES : (piece + 1) * LANES])
    pre[...] = silu_slope(pre[...])

    for part, at in enumerate(parts):
        for side_of in range(2):
            firsts[part * 2 + side_of].wait_recv()
            total = err[side_of, at] + first_in[side_of, at].astype(F32)
            err[side_of, at] = total
            second_out[side_of, at] = total.astype(BF16)
            copy = send(
                second_out.at[side_of, at],
                second_in.at[1 - side_of, at],
                sum_s.at[1, side_of, part],
                sum_r.at[1, 1 - side_of, part],
                {"mdl": mates[side_of]},
            )
            copy.start()
            seconds.append(copy)

    for copy in sums:
        copy.wait_recv()
    counts = jnp.sum(sums_in[...], axis=0)
    share = jnp.where(counts > 0.0, 2.0 / jnp.maximum(counts, 1.0), 0.0)
    weight[...] = jnp.broadcast_to(
        jnp.sum(batch_of * share[0:1, :], axis=1, keepdims=True), weight.shape
    )

    for part, at in enumerate(parts):
        for side_of in range(2):
            seconds[part * 2 + 1 - side_of].wait_recv()
            total = err[side_of, at] + second_in[side_of, at].astype(F32)
            scaled_mid[side_of, at] = (total * weight[at]).astype(BF16)
            copy = send(
                scaled_mid.at[side_of, at],
                scaled_end.at[side_of, at],
                sum_s.at[2, side_of, part],
                sum_r.at[2, side_of, part],
                {"mdl": mates[1 - side_of]},
            )
            copy.start()
            thirds.append(copy)

    def part_copy(kind, to):
        return send(
            part_out.at[kind, to],
            part_in.at[kind, me_t],
            part_s.at[kind, to],
            part_r.at[kind, me_t],
            {"teach": to},
        )

    per = teachers // 4
    part_rows = part_out.shape[2]
    back = jnp.zeros((used, up.shape[1]), F32)
    for turn, role in enumerate((1, 2, 0, 3)):
        chunk, cols, side_of = chunks[role], spans[role], turn % 2
        if turn < 2:
            scaled = scaled_mid[side_of]
        else:
            for part in range(PARTS):
                thirds[part * 2 + side_of].wait_recv()
            scaled = scaled_end[side_of]
        grad = dot(scaled, act[...], 0, 0)
        part_out[1, pl.ds(chunk * per, per)] = grad.astype(BF16).reshape(per, part_rows, -1)
        back += dot(scaled, down[cols, :])
        for piece in range(per):
            to = chunk * per + piece

            @pl.when(to != me_t)
            def _():
                part_copy(1, to).start()

    pre_grad = (back * pre[...]).astype(BF16)
    for turn in (2, 1, 3, 0):
        block = (my_x + turn * side // 4) % 4
        cols = pl.ds(pl.multiple_of(block * LANES, LANES), LANES)
        grad = dot(x[:, cols], pre_grad, 0, 0)
        part_out[0, pl.ds(block * per, per)] = grad.astype(BF16).reshape(per, part_rows, -1)
        for piece in range(per):
            to = block * per + (my_y + piece) % per

            @pl.when(to != me_t)
            def _():
                part_copy(0, to).start()

    part_in[1, me_t] = part_out[1, me_t]
    part_in[0, me_t] = part_out[0, me_t]

    def part_wait(kind):
        for step in steps:
            source = peer(step)
            send(
                part_out.at[kind, source],
                part_in.at[kind, source],
                part_s.at[kind, source],
                part_r.at[kind, source],
                {"teach": source},
            ).wait_recv()
        return jnp.sum(part_in[kind].astype(F32), axis=0)

    chips = studs // 2
    sum_down = part_wait(1).reshape(chips, part_rows // chips, -1)
    sum_up = part_wait(0).reshape(chips, part_rows // chips, -1)
    mine = grads.shape[0] // 2
    for core in range(2):
        at = slice(core * mine, (core + 1) * mine)
        rows8 = jnp.concatenate([sum_up[:, at], sum_down[:, at]], axis=1)
        last_out[:, core] = jnp.concatenate(
            [rows8[:, :, :LANES], rows8[:, :, LANES:]], axis=1
        ).astype(BF16)
    lasts = []
    for step in range(1, studs):
        to = (me_s + step) % studs
        copy = send(
            last_out.at[to // 2, to % 2],
            last_in.at[me_s],
            last_s.at[step],
            last_r.at[step],
            {"stud": to},
        )
        copy.start()
        lasts.append(copy)
    last_in[me_s] = last_out[me_s // 2, me_s % 2]
    for copy in lasts:
        copy.wait_recv()
    total = jnp.sum(last_in[...].astype(F32), axis=0)
    grads[:, :LANES] = total[: 2 * mine]
    grads[:, LANES:] = total[2 * mine :]

    for copy in going + hists + sums + firsts + seconds + thirds + lasts:
        copy.wait_send()
    for step in steps:
        for kind in range(2):
            part_copy(kind, peer(step)).wait_send()


def solution(mesh):
    teachers, studs = mesh.shape["teach"], mesh.shape["stud"]
    side = math.isqrt(teachers)

    def on_device(states, tasks, batches, teach_in, teach_out, up, down):
        width, part = up.shape
        actions = down.shape[0]
        slots, used = teachers * BLOCK, teachers * ROOM
        mine = width // (teachers * studs)
        vmem = pl.BlockSpec(memory_space=pltpu.VMEM)
        dma = pltpu.SemaphoreType.DMA
        hbm = pl.BlockSpec(memory_space=pl.ANY)
        grads = pl.pallas_call(
            functools.partial(kernel, side, teachers, studs),
            out_shape=pltpu.VMEM((2 * mine, part), F32),
            in_specs=[hbm] * 7,
            out_specs=vmem,
            scratch_shapes=[
                pltpu.VMEM((1, states.shape[0]), I32),
                pltpu.VMEM((1, states.shape[0]), I32),
                pltpu.VMEM(states.shape, BF16),
                pltpu.VMEM(teach_in.shape, BF16),
                pltpu.VMEM(teach_out.shape, BF16),
                pltpu.VMEM(up.shape, BF16),
                pltpu.VMEM(down.shape, BF16),
                pltpu.VMEM((teachers, BLOCK, width), BF16),
                pltpu.VMEM((teachers, BLOCK, width), BF16),
                pltpu.VMEM((used, width), BF16),
                pltpu.VMEM((used, part), BF16),
                pltpu.VMEM((used, part), BF16),
                pltpu.VMEM((used, part), F32),
                pltpu.VMEM((2, used, actions // 4), F32),
                pltpu.VMEM((2, used, actions // 4), BF16),
                pltpu.VMEM((2, used, actions // 4), BF16),
                pltpu.VMEM((2, used, actions // 4), BF16),
                pltpu.VMEM((2, used, actions // 4), BF16),
                pltpu.VMEM((2, used, actions // 4), BF16),
                pltpu.VMEM((2, used, actions // 4), BF16),
                pltpu.VMEM((used, LANES), F32),
                pltpu.VMEM((8, LANES), F32),
                pltpu.VMEM((studs, 8, LANES), F32),
                pltpu.VMEM((8, LANES), F32),
                pltpu.VMEM((teachers, 8, LANES), F32),
                pltpu.VMEM((2, teachers, width // teachers, part), BF16),
                pltpu.VMEM((2, teachers, width // teachers, part), BF16),
                pltpu.VMEM((studs // 2, 2, 4 * mine, part // 2), BF16),
                pltpu.VMEM((studs, 4 * mine, part // 2), BF16),
                dma((7,)),
                dma((teachers,)),
                dma((teachers,)),
                dma((3, 2, PARTS)),
                dma((3, 2, PARTS)),
                dma((studs,)),
                dma((studs,)),
                dma((teachers,)),
                dma((teachers,)),
                dma((2, teachers)),
                dma((2, teachers)),
                dma((studs,)),
                dma((studs,)),
            ],
            compiler_params=pltpu.CompilerParams(collective_id=0, has_side_effects=True),
        )(
            states,
            tasks.reshape(1, -1),
            batches.reshape(1, -1),
            teach_in,
            teach_out,
            up,
            down,
        )
        return grads[:mine], grads[mine:]

    in_specs = (
        P(("teach", "stud"), None),
        P(("teach", "stud"), None),
        P(("teach", "stud"), None),
        P("teach", None, "mdl"),
        P("teach", "mdl", None),
        P(None, "mdl"),
        P(None, "mdl"),
    )
    out_specs = (P(("teach", "stud"), "mdl"), P(("teach", "stud"), "mdl"))
    return jax.shard_map(
        on_device, mesh=mesh, in_specs=in_specs, out_specs=out_specs, check_vma=False
    )
```

```python
import functools
import math

import jax
import jax.numpy as jnp
from jax import lax
from jax.experimental import pallas as pl
from jax.experimental.pallas import tpu as pltpu
from jax.sharding import PartitionSpec as P

MESH = pl.DeviceIdType.MESH
F32, BF16, I32 = jnp.float32, jnp.bfloat16, jnp.int32
ROOM = 12
BLOCK = 16
LANES = 128
PARTS = 4


def dot(a, b, ca=1, cb=0):
    return lax.dot_general(a, b, (((ca,), (cb,)), ((), ())), preferred_element_type=F32)


def iota(shape, dim):
    return lax.broadcasted_iota(I32, shape, dim)


def onehot(mask):
    return jnp.where(mask, 1.0, 0.0).astype(BF16)


def silu(value):
    return value * jax.nn.sigmoid(value)


def silu_slope(value):
    sig = jax.nn.sigmoid(value)
    return sig * (1.0 + value * (1.0 - sig))


def kernel(
    side,
    teachers,
    studs,
    states_hbm,
    tasks_hbm,
    batches_hbm,
    teach_in_hbm,
    teach_out_hbm,
    up_hbm,
    down_hbm,
    grads,
    tasks,
    batches,
    states,
    teach_in,
    teach_out,
    up,
    down,
    out,
    got,
    x,
    hid,
    act,
    pre,
    err,
    first_out,
    first_in,
    second_out,
    second_in,
    scaled_mid,
    scaled_end,
    weight,
    hist_out,
    hist_in,
    sums_out,
    sums_in,
    part_out,
    part_in,
    last_out,
    last_in,
    load_s,
    go_s,
    go_r,
    sum_s,
    sum_r,
    hist_s,
    hist_r,
    sums_s,
    sums_r,
    part_s,
    part_r,
    last_s,
    last_r,
):
    me_t, me_s, me_m = lax.axis_index("teach"), lax.axis_index("stud"), lax.axis_index("mdl")
    my_x, my_y = me_t // side, me_t % side
    rows, width = states.shape
    slots, used = teachers * BLOCK, teachers * ROOM
    pieces = width // LANES
    mates = ((me_m + 1) % 4, (me_m + 3) % 4)

    def hops(step):
        dx, dy = step // side, step % side
        return min(dx, side - dx) + min(dy, side - dy)

    steps = sorted(range(1, teachers), key=lambda step: -hops(step))

    def peer(step):
        return ((my_x + step // side) % side) * side + (my_y + step % side) % side

    barrier = pltpu.get_barrier_semaphore()
    for step in steps:
        pl.semaphore_signal(barrier, inc=1, device_id={"teach": peer(step)}, device_id_type=MESH)
    for step in range(1, studs):
        pl.semaphore_signal(
            barrier, inc=1, device_id={"stud": (me_s + step) % studs}, device_id_type=MESH
        )
    for mate in mates:
        pl.semaphore_signal(barrier, inc=1, device_id={"mdl": mate}, device_id_type=MESH)

    def send(src, dst, send_sem, recv_sem, where):
        copy = pltpu.make_async_remote_copy(
            src_ref=src,
            dst_ref=dst,
            send_sem=send_sem,
            recv_sem=recv_sem,
            device_id=where,
            device_id_type=MESH,
        )
        return copy

    loads = []
    for index, (source, held) in enumerate(
        (
            (tasks_hbm, tasks),
            (batches_hbm, batches),
            (states_hbm, states),
            (teach_in_hbm, teach_in),
            (up_hbm, up),
            (down_hbm, down),
            (teach_out_hbm, teach_out),
        )
    ):
        loads.append(pltpu.make_async_copy(source, held, load_s.at[index]))
    for load in loads[:3]:
        load.start()

    earlier = onehot(iota((rows, rows), 0) < iota((rows, rows), 1))
    place = iota((slots, rows), 0)
    for load in loads[:2]:
        load.wait()

    hot = jnp.where(tasks[...] == iota((teachers, rows), 0), 1.0, 0.0)
    before = jnp.sum(dot(hot.astype(BF16), earlier) * hot, axis=0, keepdims=True)
    slot = tasks[...] * BLOCK + before.astype(I32)
    note = ((slot >> 4) * BLOCK + ROOM + 1 + ((slot & 15) >> 2)) * 4 + (slot & 3)
    batch_hot = onehot(batches[...] == iota((LANES, rows), 0))
    hist_out[...] = dot(jnp.ones((8, rows), BF16), batch_hot, 1, 1)
    dispatch = onehot(place == slot)
    loads[2].wait()
    for load in loads[3:]:
        load.start()
    for piece in range(pieces):
        noted = place * 4 + piece == note
        cols = slice(piece * LANES, (piece + 1) * LANES)
        block = dot(dispatch, states[:, cols]) + dot(onehot(noted), batch_hot, 1, 1)
        out[:, :, cols] = block.astype(BF16).reshape(teachers, BLOCK, LANES)

    pl.semaphore_wait(barrier, teachers - 1 + studs - 1 + 2)

    going = []
    for step in steps:
        to = peer(step)
        copy = send(
            out.at[to], got.at[me_t], go_s.at[step], go_r.at[step], {"teach": to}
        )
        copy.start()
        going.append(copy)
    got[me_t] = out[me_t]
    hists = []
    for step in range(1, studs):
        to = (me_s + step) % studs
        copy = send(
            hist_out, hist_in.at[me_s], hist_s.at[step], hist_r.at[step], {"stud": to}
        )
        copy.start()
        hists.append(copy)
    hist_in[me_s] = hist_out[...]

    source = iota((used, slots), 1)
    target = iota((used, slots), 0)
    base, inner = (source >> 4) * ROOM, source & 15
    keep = onehot((target == base + inner) & (inner < ROOM))

    for copy in going:
        copy.wait_recv()

    arrived = got[...].reshape(slots, width)

    for load in loads[3:]:
        load.wait()
    x[...] = dot(keep, arrived).astype(BF16)
    hid[...] = silu(dot(x[...], teach_in[0])).astype(BF16)
    pre[...] = dot(x[...], up[...])
    act[...] = silu(pre[...]).astype(BF16)

    chunks, spans = [], []
    for role in range(4):
        chunks.append((me_m + 4 - role + my_x * 4 // side) % 4)
        spans.append(pl.ds(pl.multiple_of(chunks[role] * LANES, LANES), LANES))

    def diff(role):
        cols = spans[role]
        return dot(act[...], down[cols, :], 1, 1) - dot(hid[...], teach_out[0, :, cols])

    parts = [slice(part * used // PARTS, (part + 1) * used // PARTS) for part in range(PARTS)]
    firsts, seconds, thirds = [], [], []
    for side_of, role in enumerate((0, 3)):
        first_out[side_of] = diff(role).astype(BF16)
        for part, at in enumerate(parts):
            copy = send(
                first_out.at[side_of, at],
                first_in.at[side_of, at],
                sum_s.at[0, side_of, part],
                sum_r.at[0, side_of, part],
                {"mdl": mates[side_of]},
            )
            copy.start()
            firsts.append(copy)
    for side_of, role in enumerate((1, 2)):
        err[side_of] = diff(role)

    for copy in hists:
        copy.wait_recv()
    sums_out[...] = jnp.sum(hist_in[...], axis=0)
    sums = []
    for step in steps:
        copy = send(
            sums_out, sums_in.at[me_t], sums_s.at[step], sums_r.at[step], {"teach": peer(step)}
        )
        copy.start()
        sums.append(copy)
    sums_in[me_t] = sums_out[...]
    batch_of = jnp.zeros((used, LANES), F32)
    for piece in range(pieces):
        pick = onehot((target == base + (inner - ROOM - 1) * 4 + piece) & (inner > ROOM))
        batch_of += dot(pick, arrived[:, piece * LANES : (piece + 1) * LANES])
    pre[...] = silu_slope(pre[...])

    for part, at in enumerate(parts):
        for side_of in range(2):
            firsts[side_of * PARTS + part].wait_recv()
            total = err[side_of, at] + first_in[side_of, at].astype(F32)
            err[side_of, at] = total
            second_out[side_of, at] = total.astype(BF16)
            copy = send(
                second_out.at[side_of, at],
                second_in.at[1 - side_of, at],
                sum_s.at[1, side_of, part],
                sum_r.at[1, 1 - side_of, part],
                {"mdl": mates[side_of]},
            )
            copy.start()
            seconds.append(copy)

    for copy in sums:
        copy.wait_recv()
    counts = jnp.sum(sums_in[...], axis=0)
    share = jnp.where(counts > 0.0, 2.0 / jnp.maximum(counts, 1.0), 0.0)
    weight[...] = jnp.broadcast_to(
        jnp.sum(batch_of * share[0:1, :], axis=1, keepdims=True), weight.shape
    )

    for part, at in enumerate(parts):
        for side_of in range(2):
            seconds[part * 2 + 1 - side_of].wait_recv()
            total = err[side_of, at] + second_in[side_of, at].astype(F32)
            scaled_mid[side_of, at] = (total * weight[at]).astype(BF16)
            copy = send(
                scaled_mid.at[side_of, at],
                scaled_end.at[side_of, at],
                sum_s.at[2, side_of, part],
                sum_r.at[2, side_of, part],
                {"mdl": mates[1 - side_of]},
            )
            copy.start()
            thirds.append(copy)

    def part_copy(kind, to):
        return send(
            part_out.at[kind, to],
            part_in.at[kind, me_t],
            part_s.at[kind, to],
            part_r.at[kind, me_t],
            {"teach": to},
        )

    per = teachers // 4
    part_rows = part_out.shape[2]
    back = jnp.zeros((used, up.shape[1]), F32)
    for turn, role in enumerate((1, 2, 0, 3)):
        chunk, cols, side_of = chunks[role], spans[role], turn % 2
        if turn < 2:
            scaled = scaled_mid[side_of]
        else:
            for part in range(PARTS):
                thirds[part * 2 + side_of].wait_recv()
            scaled = scaled_end[side_of]
        grad = dot(scaled, act[...], 0, 0)
        part_out[1, pl.ds(chunk * per, per)] = grad.astype(BF16).reshape(per, part_rows, -1)
        back += dot(scaled, down[cols, :])
        for piece in range(per):
            to = chunk * per + piece

            @pl.when(to != me_t)
            def _():
                part_copy(1, to).start()

    pre_grad = (back * pre[...]).astype(BF16)
    for turn in (2, 1, 3, 0):
        block = (my_x + turn * side // 4) % 4
        cols = pl.ds(pl.multiple_of(block * LANES, LANES), LANES)
        grad = dot(x[:, cols], pre_grad, 0, 0)
        part_out[0, pl.ds(block * per, per)] = grad.astype(BF16).reshape(per, part_rows, -1)
        for piece in range(per):
            to = block * per + (my_y + piece) % per

            @pl.when(to != me_t)
            def _():
                part_copy(0, to).start()

    part_in[1, me_t] = part_out[1, me_t]
    part_in[0, me_t] = part_out[0, me_t]

    def part_wait(kind):
        for step in steps:
            source = peer(step)
            send(
                part_out.at[kind, source],
                part_in.at[kind, source],
                part_s.at[kind, source],
                part_r.at[kind, source],
                {"teach": source},
            ).wait_recv()
        return jnp.sum(part_in[kind].astype(F32), axis=0)

    chips = studs // 2
    sum_down = part_wait(1).reshape(chips, part_rows // chips, -1)
    sum_up = part_wait(0).reshape(chips, part_rows // chips, -1)
    mine = grads.shape[0] // 2
    for core in range(2):
        at = slice(core * mine, (core + 1) * mine)
        rows8 = jnp.concatenate([sum_up[:, at], sum_down[:, at]], axis=1)
        last_out[:, core] = jnp.concatenate(
            [rows8[:, :, :LANES], rows8[:, :, LANES:]], axis=1
        ).astype(BF16)
    lasts = []
    for step in range(1, studs):
        to = (me_s + step) % studs
        copy = send(
            last_out.at[to // 2, to % 2],
            last_in.at[me_s],
            last_s.at[step],
            last_r.at[step],
            {"stud": to},
        )
        copy.start()
        lasts.append(copy)
    last_in[me_s] = last_out[me_s // 2, me_s % 2]
    for copy in lasts:
        copy.wait_recv()
    total = jnp.sum(last_in[...].astype(F32), axis=0)
    grads[:, :LANES] = total[: 2 * mine]
    grads[:, LANES:] = total[2 * mine :]

    for copy in going + hists + sums + firsts + seconds + thirds + lasts:
        copy.wait_send()
    for step in steps:
        for kind in range(2):
            part_copy(kind, peer(step)).wait_send()


def solution(mesh):
    teachers, studs = mesh.shape["teach"], mesh.shape["stud"]
    side = math.isqrt(teachers)

    def on_device(states, tasks, batches, teach_in, teach_out, up, down):
        width, part = up.shape
        actions = down.shape[0]
        slots, used = teachers * BLOCK, teachers * ROOM
        mine = width // (teachers * studs)
        vmem = pl.BlockSpec(memory_space=pltpu.VMEM)
        dma = pltpu.SemaphoreType.DMA
        hbm = pl.BlockSpec(memory_space=pl.ANY)
        grads = pl.pallas_call(
            functools.partial(kernel, side, teachers, studs),
            out_shape=pltpu.VMEM((2 * mine, part), F32),
            in_specs=[hbm] * 7,
            out_specs=vmem,
            scratch_shapes=[
                pltpu.VMEM((1, states.shape[0]), I32),
                pltpu.VMEM((1, states.shape[0]), I32),
                pltpu.VMEM(states.shape, BF16),
                pltpu.VMEM(teach_in.shape, BF16),
                pltpu.VMEM(teach_out.shape, BF16),
                pltpu.VMEM(up.shape, BF16),
                pltpu.VMEM(down.shape, BF16),
                pltpu.VMEM((teachers, BLOCK, width), BF16),
                pltpu.VMEM((teachers, BLOCK, width), BF16),
                pltpu.VMEM((used, width), BF16),
                pltpu.VMEM((used, part), BF16),
                pltpu.VMEM((used, part), BF16),
                pltpu.VMEM((used, part), F32),
                pltpu.VMEM((2, used, actions // 4), F32),
                pltpu.VMEM((2, used, actions // 4), BF16),
                pltpu.VMEM((2, used, actions // 4), BF16),
                pltpu.VMEM((2, used, actions // 4), BF16),
                pltpu.VMEM((2, used, actions // 4), BF16),
                pltpu.VMEM((2, used, actions // 4), BF16),
                pltpu.VMEM((2, used, actions // 4), BF16),
                pltpu.VMEM((used, LANES), F32),
                pltpu.VMEM((8, LANES), F32),
                pltpu.VMEM((studs, 8, LANES), F32),
                pltpu.VMEM((8, LANES), F32),
                pltpu.VMEM((teachers, 8, LANES), F32),
                pltpu.VMEM((2, teachers, width // teachers, part), BF16),
                pltpu.VMEM((2, teachers, width // teachers, part), BF16),
                pltpu.VMEM((studs // 2, 2, 4 * mine, part // 2), BF16),
                pltpu.VMEM((studs, 4 * mine, part // 2), BF16),
                dma((7,)),
                dma((teachers,)),
                dma((teachers,)),
                dma((3, 2, PARTS)),
                dma((3, 2, PARTS)),
                dma((studs,)),
                dma((studs,)),
                dma((teachers,)),
                dma((teachers,)),
                dma((2, teachers)),
                dma((2, teachers)),
                dma((studs,)),
                dma((studs,)),
            ],
            compiler_params=pltpu.CompilerParams(collective_id=0, has_side_effects=True),
        )(
            states,
            tasks.reshape(1, -1),
            batches.reshape(1, -1),
            teach_in,
            teach_out,
            up,
            down,
        )
        return grads[:mine], grads[mine:]

    in_specs = (
        P(("teach", "stud"), None),
        P(("teach", "stud"), None),
        P(("teach", "stud"), None),
        P("teach", None, "mdl"),
        P("teach", "mdl", None),
        P(None, "mdl"),
        P(None, "mdl"),
    )
    out_specs = (P(("teach", "stud"), "mdl"), P(("teach", "stud"), "mdl"))
    return jax.shard_map(
        on_device, mesh=mesh, in_specs=in_specs, out_specs=out_specs, check_vma=False
    )
```
